32 devices in a mesh: dp: 2 (over x), row: 4 (over z), col: 4 (over y, core).
Axes of the slice: x: 2, y: 2, z: 4, core: 2. Of those that a mesh axis runs over, the one named last changes fastest.
Arguments:
- block_input: bfloat16 [4096, 2304], P(('dp', 'col'), 'row'), may hold values from -6 to 6
- query_weight: bfloat16 [2304, 2048], P('row', 'col'), may hold values from -0.125 to 0.125
- key_matrix: bfloat16 [2304, 1024], P('row', 'col'), may hold values from -0.125 to 0.125
- value_matrix: bfloat16 [2304, 1024], P('row', 'col'), may hold values from -0.125 to 0.125
- output_weight: bfloat16 [2048, 2304], P('col', 'row'), may hold values from -0.125 to 0.125
- gate_weight: bfloat16 [2304, 9216], P('row', 'col'), may hold values from -0.125 to 0.125
- up_weight: bfloat16 [2304, 9216], P('row', 'col'), may hold values from -0.125 to 0.125
- down_weight: bfloat16 [9216, 2304], P('col', 'row'), may hold values from -0.0625 to 0.0625
- norm_gains: float32 [4, 2304], P(None, 'row'), may hold values from -0.5 to 0.5
- segment_ids: int32 [4096], P(('dp', 'row')), may hold values from 0 to 9, never falling along the last dimension, each value on 1 to 2000 neighbouring positions
- positions: int32 [4096], P(('dp', 'row')), may hold values from 0 to 8191
- cotangent: bfloat16 [4096, 2304], P(('dp', 'col'), 'row'), may hold values from -6 to 6
Outputs:
- layer_output: bfloat16 [4096, 2304], P(('dp', 'col'), 'row')
- input_grad: float32 [4096, 2304], P(('dp', 'col'), 'row')
- query_grad: float32 [2304, 2048], P('row', 'col')
- key_grad: float32 [2304, 1024], P('row', 'col')
- value_grad: float32 [2304, 1024], P('row', 'col')
- output_grad: float32 [2048, 2304], P('col', 'row')
- gate_grad: float32 [2304, 9216], P('row', 'col')
- up_grad: float32 [2304, 9216], P('row', 'col')
- down_grad: float32 [9216, 2304], P('col', 'row')
- gains_grad: float32 [4, 2304], P(None, 'row')
The draws below stay inside these ranges and needn't reach their ends.
Inputs may be any that keep to these rules, and one draw needn't show every extreme that they name: `segment_ids`: segment numbers never fall from one token to the next.
All inputs are finite; a program needn't handle non-finite values.
Results may differ from the reference program's by a relative error of at most 0.024.
Values may be sent and summed in bfloat16 or wider, within the bound.
No kernel may reach another device: no remote copies, remote signals or barrier semaphores. Data moves between devices by JAX's collectives and lax.ppermute only.
A program may use at most 192 MiB of HBM per device.

```python
import math
import jax
import jax.numpy as jnp
import numpy as np
from jax import lax

MODEL_WIDTH = 2304
QUERY_HEADS = 8
KEY_VALUE_HEADS = 4
HEAD_WIDTH = 256
FF = 9216
SEQUENCE_LENGTH = 512
TOKENS = 4096


def place_ends(drawn, rng, low, top_value):
    shape = drawn.shape
    index_at = [jax.random.randint(jax.random.fold_in(rng, axis), (), 0, shape[axis]) for axis in range(len(shape))]
    drawn = drawn.at[tuple(index_at)].set(low)
    longest = shape.index(max(shape))
    index_at[longest] = (index_at[longest] + 1) % shape[longest]
    return drawn.at[tuple(index_at)].set(top_value)


def shard_levels(own_key, dims, cuts, low, high):
    loudness, own = 1.0, jax.random.fold_in(own_key, 6)
    for position, parts in cuts:
        steps = jnp.exp(jax.random.uniform(jax.random.fold_in(own, position), (parts,), jnp.float32, low / len(cuts), high / len(cuts)))
        loudness = loudness * jnp.repeat(steps, dims[position] // parts).reshape([-1 if axis == position else 1 for axis in range(len(dims))])
    return loudness


def length_profile(count, total, bound, slope):
    loads = [(1 << 20) // math.isqrt(grade ** slope) + 1 for grade in range(2, count + 1)]
    spare, holding = total - bound - (count - 1), [1] * (count - 1)
    while spare > 0:
        candidates = [i for i in range(count - 1) if holding[i] < bound]
        whole, left = sum([loads[i] for i in candidates]), spare
        for i in candidates:
            extra = min(bound - holding[i], max(1, left * loads[i] // whole), spare)
            holding[i] = holding[i] + extra
            spare = spare - extra
    return np.array([bound] + holding)


def ragged(rng, amount, total, reach, slope):
    if amount == 2:
        one = jax.random.randint(rng, (), max(1, total - reach), min(reach, total - 1) + 1)
        return jnp.stack([one, total - one])
    lengths = jnp.asarray(length_profile(amount, total, reach, slope), jnp.int32)
    twos = (amount - 1) // 2
    donor, receiver = lengths[1:1 + 2 * twos:2], lengths[2:2 + 2 * twos:2]
    room = jnp.minimum(donor - 1, reach - receiver)
    passed = jax.random.randint(jax.random.fold_in(rng, 1), (twos,), 0, 1 << 20) % (room + 1)
    lengths = lengths.at[1:1 + 2 * twos:2].set(donor - passed).at[2:2 + 2 * twos:2].set(receiver + passed)
    return lengths[jax.random.permutation(jax.random.fold_in(rng, 2), amount)]


def normal_values(key, dims, deviation, most, split=(), held_as=jnp.bfloat16):
    values = jax.random.normal(key, dims, jnp.float32) * deviation
    if len(split) > 0:
        values = shard_levels(key, dims, split, -0.22, 0.18) * values
    return jnp.clip(values, min=-most, max=most).astype(held_as)


def setup_inputs(seed: int = 0) -> dict:
    key_of = jax.random.split(jax.random.key(seed), 13)
    return {
        "block_input": normal_values(key_of[0], (TOKENS, MODEL_WIDTH), 1.0, 6.0, ((0, 8), (1, 4))),
        "query_weight": normal_values(key_of[1], (MODEL_WIDTH, QUERY_HEADS * HEAD_WIDTH), MODEL_WIDTH ** -0.5, 0.125, ((0, 4), (1, 4))),
        "key_matrix": normal_values(key_of[2], (MODEL_WIDTH, KEY_VALUE_HEADS * HEAD_WIDTH), MODEL_WIDTH ** -0.5, 0.125, ((0, 4), (1, 4))),
        "value_matrix": normal_values(key_of[3], (MODEL_WIDTH, KEY_VALUE_HEADS * HEAD_WIDTH), MODEL_WIDTH ** -0.5, 0.125, ((0, 4), (1, 4))),
        "output_weight": normal_values(key_of[4], (QUERY_HEADS * HEAD_WIDTH, MODEL_WIDTH), (QUERY_HEADS * HEAD_WIDTH) ** -0.5, 0.125, ((0, 4), (1, 4))),
        "gate_weight": normal_values(key_of[5], (MODEL_WIDTH, FF), MODEL_WIDTH ** -0.5, 0.125, ((0, 4), (1, 4))),
        "up_weight": normal_values(key_of[6], (MODEL_WIDTH, FF), MODEL_WIDTH ** -0.5, 0.125, ((0, 4), (1, 4))),
        "down_weight": normal_values(key_of[7], (FF, MODEL_WIDTH), FF ** -0.5, 0.0625, ((0, 4), (1, 4))),
        "norm_gains": jnp.clip(jax.random.uniform(key_of[8], (4, MODEL_WIDTH), jnp.float32, -0.5, 0.5) * shard_levels(key_of[8], (4, MODEL_WIDTH), ((1, 4),), -0.4, 0.0), -0.5, 0.5),
        "segment_ids": jnp.searchsorted(jnp.cumsum(ragged(key_of[9], max(3, TOKENS // 400), TOKENS, min(2000, TOKENS // 2), 0)), jnp.arange(TOKENS), side="right").astype(jnp.int32),
        "positions": place_ends(jax.random.randint(key_of[10], (TOKENS,), 0, 8192), jax.random.fold_in(key_of[10], 1), 0, 8191).astype(jnp.int32),
        "cotangent": normal_values(key_of[11], (TOKENS, MODEL_WIDTH), 1.0, 6.0, ((0, 8), (1, 4))),
    }


EPSILON = 1e-06
SOFT_CAP = 50.0

def norm_forward(values, gain):
    inverse = lax.rsqrt(lax.optimization_barrier(jnp.mean(values * values, axis=-1, keepdims=True)) + EPSILON)
    return (values * inverse * (1.0 + gain), inverse)

def norm_backward(values, inverse, gain, grad):
    normed = values * inverse
    scaled = grad * (1.0 + gain)
    result = inverse * (scaled - normed * lax.optimization_barrier(jnp.mean(scaled * normed, axis=-1, keepdims=True)))
    return (result, lax.optimization_barrier(jnp.sum(grad * normed, axis=0)))

def gelu_tanh(values):
    return jax.nn.gelu(values, approximate=True)

def rope_tables(positions):
    halfway = HEAD_WIDTH // 2
    frequency = jnp.exp(jnp.arange(halfway, dtype=jnp.float32) * (-2.0 * math.log(10000.0) / HEAD_WIDTH))
    angles = positions.astype(jnp.float32)[:, None] * frequency[None, :]
    return (jnp.cos(angles)[:, None, :], jnp.sin(angles)[:, None, :])

def apply_rotary(values, cosine_table, sine_table):
    halfway = values.shape[-1] // 2
    lower_half = values[..., :halfway]
    upper_half = values[..., halfway:]
    return jnp.concatenate([lower_half * cosine_table - upper_half * sine_table, upper_half * cosine_table + lower_half * sine_table], axis=-1)

def reverse_rotary(values, cosine_table, sine_table):
    halfway = values.shape[-1] // 2
    lower_half = values[..., :halfway]
    upper_half = values[..., halfway:]
    return jnp.concatenate([lower_half * cosine_table + upper_half * sine_table, upper_half * cosine_table - lower_half * sine_table], axis=-1)

def visible(segments):
    seq_length = segments.shape[-1]
    ordinal = jnp.arange(seq_length)
    causal = ordinal[None, :] <= ordinal[:, None]
    same_doc = segments[:, :, None] == segments[:, None, :]
    return (same_doc & causal[None])[:, None, None]

def attend_forward(queries, keys, values, segments):
    scores = jnp.einsum('sqkge,stke->skgqt', queries.astype(jnp.float32), keys.astype(jnp.float32))
    capped = SOFT_CAP * jnp.tanh(scores / SOFT_CAP)
    allowed = visible(segments)
    totals = lax.optimization_barrier(jnp.sum(jnp.where(allowed, jnp.exp(capped), 0.0), axis=-1, keepdims=True))
    logsum = jnp.log(totals)
    probs_low = jnp.where(allowed, jnp.exp(capped - logsum), 0.0).astype(jnp.bfloat16)
    outputs = jnp.einsum('skgqt,stke->sqkge', probs_low.astype(jnp.float32), values.astype(jnp.float32))
    return (outputs.astype(jnp.bfloat16), logsum)

def attend_backward(queries, keys, values, segments, logsum, grad_out):
    scores = jnp.einsum('sqkge,stke->skgqt', queries.astype(jnp.float32), keys.astype(jnp.float32))
    capped = SOFT_CAP * jnp.tanh(scores / SOFT_CAP)
    allowed = visible(segments)
    probs = jnp.where(allowed, jnp.exp(capped - logsum), 0.0)
    probs_low = probs.astype(jnp.bfloat16)
    grad_probs = jnp.einsum('sqkge,stke->skgqt', grad_out.astype(jnp.float32), values.astype(jnp.float32))
    centre = lax.optimization_barrier(jnp.sum(probs * grad_probs, axis=-1, keepdims=True))
    squash = capped / SOFT_CAP
    grad_scores = (probs * (grad_probs - centre) * (1.0 - squash * squash)).astype(jnp.bfloat16)
    grad_q = jnp.einsum('skgqt,stke->sqkge', grad_scores.astype(jnp.float32), keys.astype(jnp.float32))
    key_gradient = jnp.einsum('skgqt,sqkge->stke', grad_scores.astype(jnp.float32), queries.astype(jnp.float32))
    value_gradient = jnp.einsum('skgqt,sqkge->stke', probs_low.astype(jnp.float32), grad_out.astype(jnp.float32))
    return (grad_q, key_gradient, value_gradient)

def product(left, right):
    return jnp.dot(left, right, preferred_element_type=jnp.float32)

def layer_rows(inputs_rows, cot_rows, seg_rows, pos_rows, weights):
    query_weight, key_matrix, value_matrix, output_weight, gate_weight, up_weight, down_weight, norm_gains = weights
    total_rows = inputs_rows.shape[0]
    sequence_count = total_rows // SEQUENCE_LENGTH
    query_group_width = QUERY_HEADS // KEY_VALUE_HEADS
    scale = HEAD_WIDTH ** (-0.5)
    residual = inputs_rows.astype(jnp.float32)
    normed_one, inverse_one = norm_forward(residual, norm_gains[0])
    act_one = normed_one.astype(jnp.bfloat16)
    query = product(act_one, query_weight)
    unrotated_key = product(act_one, key_matrix)
    value_raw = product(act_one, value_matrix)
    cosine_table, sine_table = rope_tables(pos_rows)
    rotated_query = (apply_rotary(query.reshape(total_rows, QUERY_HEADS, HEAD_WIDTH), cosine_table, sine_table) * scale).astype(jnp.bfloat16)
    rotated_key = apply_rotary(unrotated_key.reshape(total_rows, KEY_VALUE_HEADS, HEAD_WIDTH), cosine_table, sine_table).astype(jnp.bfloat16)
    value_reduced = value_raw.astype(jnp.bfloat16)
    reshaped_queries = rotated_query.reshape(sequence_count, SEQUENCE_LENGTH, KEY_VALUE_HEADS, query_group_width, HEAD_WIDTH)
    reshaped_keys = rotated_key.reshape(sequence_count, SEQUENCE_LENGTH, KEY_VALUE_HEADS, HEAD_WIDTH)
    reshaped_values = value_reduced.reshape(sequence_count, SEQUENCE_LENGTH, KEY_VALUE_HEADS, HEAD_WIDTH)
    seg_shaped = seg_rows.reshape(sequence_count, SEQUENCE_LENGTH)
    attended, logsum = attend_forward(reshaped_queries, reshaped_keys, reshaped_values, seg_shaped)
    attended_flat = attended.reshape(total_rows, QUERY_HEADS * HEAD_WIDTH)
    branch_one = product(attended_flat, output_weight)
    post_one, inverse_b1 = norm_forward(branch_one, norm_gains[1])
    hidden_res = residual + post_one
    normed_two, inverse_two = norm_forward(hidden_res, norm_gains[2])
    act_two = normed_two.astype(jnp.bfloat16)
    gate = product(act_two, gate_weight)
    upper = product(act_two, up_weight)
    activated, gelu_back = jax.vjp(gelu_tanh, gate)
    inner = (activated * upper).astype(jnp.bfloat16)
    branch_two = product(inner, down_weight)
    post_two, inverse_b2 = norm_forward(branch_two, norm_gains[3])
    layer_out = (hidden_res + post_two).astype(jnp.bfloat16)
    grad_res = cot_rows.astype(jnp.float32)
    grad_b2, gain_three = norm_backward(branch_two, inverse_b2, norm_gains[3], grad_res)
    low_two = grad_b2.astype(jnp.bfloat16)
    grad_down = product(inner.T, low_two)
    grad_inner = product(low_two, down_weight.T)
    grad_gate_low = gelu_back(grad_inner * upper)[0].astype(jnp.bfloat16)
    grad_up_low = (grad_inner * activated).astype(jnp.bfloat16)
    grad_gate_w = product(act_two.T, grad_gate_low)
    grad_up_w = product(act_two.T, grad_up_low)
    grad_act_two = product(grad_gate_low, gate_weight.T) + product(grad_up_low, up_weight.T)
    grad_hidden, gain_two = norm_backward(hidden_res, inverse_two, norm_gains[2], grad_act_two)
    grad_hidden = grad_hidden + grad_res
    grad_b1, gain_one = norm_backward(branch_one, inverse_b1, norm_gains[1], grad_hidden)
    low_one = grad_b1.astype(jnp.bfloat16)
    grad_out_w = product(attended_flat.T, low_one)
    grad_attended = product(low_one, output_weight.T).astype(jnp.bfloat16)
    grad_q, key_gradient, value_gradient = attend_backward(reshaped_queries, reshaped_keys, reshaped_values, seg_shaped, logsum, grad_attended.reshape(reshaped_queries.shape))
    grad_query = (reverse_rotary(grad_q.reshape(total_rows, QUERY_HEADS, HEAD_WIDTH), cosine_table, sine_table) * scale).reshape(total_rows, QUERY_HEADS * HEAD_WIDTH).astype(jnp.bfloat16)
    gradient_keys = reverse_rotary(key_gradient.reshape(total_rows, KEY_VALUE_HEADS, HEAD_WIDTH), cosine_table, sine_table).reshape(total_rows, KEY_VALUE_HEADS * HEAD_WIDTH).astype(jnp.bfloat16)
    gradient_values = value_gradient.reshape(total_rows, KEY_VALUE_HEADS * HEAD_WIDTH).astype(jnp.bfloat16)
    grad_query_w = product(act_one.T, grad_query)
    grad_key_w = product(act_one.T, gradient_keys)
    grad_value_w = product(act_one.T, gradient_values)
    grad_act_one = product(grad_query, query_weight.T) + product(gradient_keys, key_matrix.T) + product(gradient_values, value_matrix.T)
    grad_input, gain_zero = norm_backward(residual, inverse_one, norm_gains[0], grad_act_one)
    grad_input = grad_input + grad_hidden
    gains_part = jnp.stack([gain_zero, gain_one, gain_two, gain_three])
    grads = (grad_query_w, grad_key_w, grad_value_w, grad_out_w, grad_gate_w, grad_up_w, grad_down, gains_part)
    return (layer_out, grad_input, grads)

def reference(block_input, query_weight, key_matrix, value_matrix, output_weight, gate_weight, up_weight, down_weight, norm_gains, segment_ids, positions, cotangent):
    total_seqs = TOKENS // SEQUENCE_LENGTH
    per_block = 1
    for candidate in range(1, max(1, 4096 // SEQUENCE_LENGTH) + 1):
        if total_seqs % candidate == 0:
            per_block = candidate
    block_rows = per_block * SEQUENCE_LENGTH
    block_count = TOKENS // block_rows
    weights = (query_weight, key_matrix, value_matrix, output_weight, gate_weight, up_weight, down_weight, norm_gains)
    initial = (jnp.zeros(query_weight.shape, jnp.float32), jnp.zeros(key_matrix.shape, jnp.float32), jnp.zeros(value_matrix.shape, jnp.float32), jnp.zeros(output_weight.shape, jnp.float32), jnp.zeros(gate_weight.shape, jnp.float32), jnp.zeros(up_weight.shape, jnp.float32), jnp.zeros(down_weight.shape, jnp.float32), jnp.zeros(norm_gains.shape, jnp.float32))

    def step_block(totals, pieces):
        inputs_rows, cot_rows, seg_rows, pos_rows = pieces
        layer_out, grad_input, grads = layer_rows(inputs_rows, cot_rows, seg_rows, pos_rows, weights)
        updated = tuple((earlier + latest for earlier, latest in zip(totals, grads)))
        return (updated, (layer_out, grad_input))
    stacked = (block_input.reshape(block_count, block_rows, MODEL_WIDTH), cotangent.reshape(block_count, block_rows, MODEL_WIDTH), segment_ids.reshape(block_count, block_rows), positions.reshape(block_count, block_rows))
    totals, (outputs, input_grads) = lax.scan(step_block, initial, stacked)
    return (outputs.reshape(TOKENS, MODEL_WIDTH), input_grads.reshape(TOKENS, MODEL_WIDTH), totals[0], totals[1], totals[2], totals[3], totals[4], totals[5], totals[6], totals[7])
```

```python
import math

import jax
import jax.numpy as jnp
from jax import lax
from jax.sharding import PartitionSpec as P

HEAD_WIDTH = 256
SEQUENCE_LENGTH = 512

EPSILON = 1e-06
SOFT_CAP = 50.0


CORE_SWAP = [(0, 1), (1, 0), (2, 3), (3, 2)]
Y_SWAP = [(0, 2), (2, 0), (1, 3), (3, 1)]


def spread_pairs(phase):
    pairs = []
    for z in range(4):
        for c in range(4):
            y, k = c >> 1, c & 1
            target = 2 * k + (phase ^ (z & 1))
            pairs.append((4 * z + c, 4 * target + 2 * y + (z >> 1)))
    return pairs


SPREAD = [spread_pairs(0), spread_pairs(1)]
COLLECT = [[(b, a) for a, b in pairs] for pairs in SPREAD]


def product(left, right):
    return jnp.dot(left, right, preferred_element_type=jnp.float32)


def product_tn(left, right):
    return lax.dot_general(left, right, (((0,), (0,)), ((), ())), preferred_element_type=jnp.float32)


def product_nt(left, right):
    return lax.dot_general(left, right, (((1,), (1,)), ((), ())), preferred_element_type=jnp.float32)


def low(values):
    return values.astype(jnp.bfloat16)


def wide(values):
    return values.astype(jnp.float32)


def ordered(flag, own, other):
    first = jnp.where(flag == 0, own, other)
    second = jnp.where(flag == 0, other, own)
    return jnp.stack([first, second])


def inverse_rms(values):
    return lax.rsqrt(jnp.mean(values * values, axis=-1, keepdims=True) + EPSILON)


def norm_backward(values, inverse, gain, grad):
    normed = values * inverse
    scaled = grad * (1.0 + gain)
    result = inverse * (scaled - normed * jnp.mean(scaled * normed, axis=-1, keepdims=True))
    return result, jnp.sum(grad * normed, axis=0)


def gelu_tanh(values):
    return jax.nn.gelu(values, approximate=True)


def rope_tables(positions):
    halfway = HEAD_WIDTH // 2
    frequency = jnp.exp(jnp.arange(halfway, dtype=jnp.float32) * (-2.0 * math.log(10000.0) / HEAD_WIDTH))
    angles = positions.astype(jnp.float32)[:, None] * frequency[None, :]
    return jnp.cos(angles), jnp.sin(angles)


def rotate(values, cosine, sine):
    halfway = HEAD_WIDTH // 2
    a, b = values[:, :halfway], values[:, halfway:]
    return jnp.concatenate([a * cosine - b * sine, b * cosine + a * sine], axis=-1)


def visible(segments):
    ordinal = jnp.arange(segments.shape[0])
    return (ordinal[None, :] <= ordinal[:, None]) & (segments[:, None] == segments[None, :])


def attend_forward(query, key, value, allowed):
    capped = SOFT_CAP * jnp.tanh(product_nt(query, key) / SOFT_CAP)
    totals = jnp.sum(jnp.where(allowed, jnp.exp(capped), 0.0), axis=-1, keepdims=True)
    logsum = jnp.log(totals)
    probs_low = low(jnp.where(allowed, jnp.exp(capped - logsum), 0.0))
    return low(product(probs_low, value)), logsum


def attend_backward(query, key, value, allowed, logsum, grad_out):
    capped = SOFT_CAP * jnp.tanh(product_nt(query, key) / SOFT_CAP)
    probs = jnp.where(allowed, jnp.exp(capped - logsum), 0.0)
    grad_probs = product_nt(grad_out, value)
    centre = jnp.sum(probs * grad_probs, axis=-1, keepdims=True)
    squash = capped / SOFT_CAP
    grad_scores = low(probs * (grad_probs - centre) * (1.0 - squash * squash))
    return product(grad_scores, key), product_tn(grad_scores, query), product_tn(low(probs), grad_out)


def make_body(dp_size):
    def place():
        c = lax.axis_index("col")
        return lax.axis_index("dp"), lax.axis_index("row"), c >> 1, c & 1

    def dp_gather(piece):
        if dp_size == 2:
            other = lax.ppermute(piece, "dp", [(0, 1), (1, 0)])
            return jnp.moveaxis(ordered(lax.axis_index("dp"), piece, other), 0, 1)
        return jnp.moveaxis(lax.all_gather(piece, "dp"), 0, 1)

    def dp_scatter(blocks):
        if dp_size == 2:
            d = lax.axis_index("dp")
            sent = lax.dynamic_index_in_dim(blocks, 1 - d, 1, keepdims=False)
            kept = lax.dynamic_index_in_dim(blocks, d, 1, keepdims=False)
            return low(wide(kept) + wide(lax.ppermute(sent, "dp", [(0, 1), (1, 0)])))
        return lax.psum_scatter(jnp.moveaxis(blocks, 1, 0), "dp", scatter_dimension=0, tiled=False)

    def spread(half_zero, half_one):
        d, z, y, k = place()
        stored, n = half_zero.shape
        rows = stored // dp_size
        halves = jnp.stack([half_zero, half_one])
        parity = z & 1
        got = []
        for phase in range(2):
            piece = lax.dynamic_slice(halves, (phase ^ parity, d * rows, 0), (1, rows, n))[0]
            got.append(lax.ppermute(piece, ("row", "col"), SPREAD[phase]))
        blocks = ordered(parity, got[0], got[1])
        blocks = dp_gather(blocks).reshape(2 * stored, n)
        whole = ordered(k, blocks, lax.ppermute(blocks, "col", CORE_SWAP)).reshape(4 * stored, n)
        return whole, lax.ppermute(whole, "col", Y_SWAP)

    def collect(own, other):
        d, z, y, k = place()
        total, n = own.shape
        stored = total // 4
        rows = stored // dp_size
        both = jnp.stack([own, other]).reshape(2, 2, 2 * stored, n)
        sent = lax.dynamic_index_in_dim(both, 1 - k, 1, keepdims=False)
        kept = lax.dynamic_index_in_dim(both, k, 1, keepdims=False)
        both = low(wide(kept) + wide(lax.ppermute(sent, "col", CORE_SWAP)))
        summed = low(wide(both[0]) + wide(lax.ppermute(both[1], "col", Y_SWAP)))
        pieces = dp_scatter(summed.reshape(2, dp_size, rows, n))
        parity = z & 1
        got = []
        for phase in range(2):
            piece = lax.dynamic_index_in_dim(pieces, phase ^ parity, 0, keepdims=False)
            got.append(lax.ppermute(piece, ("row", "col"), COLLECT[phase]))
        halves = dp_gather(ordered(parity, got[0], got[1]))
        return halves.reshape(2, stored, n)

    def body(
        block_input,
        query_weight,
        key_matrix,
        value_matrix,
        output_weight,
        gate_weight,
        up_weight,
        down_weight,
        norm_gains,
        segment_ids,
        positions,
        cotangent,
    ):
        tokens, stored = block_input.shape
        width = 4 * stored
        chunk = tokens // 4
        scale = HEAD_WIDTH ** (-0.5)
        half = gate_weight.shape[1] // 2
        d, z, y, k = place()

        def gather_rows(values):
            return lax.all_gather(low(values), "row", axis=0, tiled=True)

        def scatter_rows(values):
            return wide(lax.psum_scatter(low(values), "row", scatter_dimension=0, tiled=True))

        def to_chunks(values):
            got = lax.all_to_all(values.reshape(4, chunk, stored), "row", 0, 0)
            return got.transpose(1, 0, 2).reshape(chunk, width)

        def from_chunks(values):
            got = lax.all_to_all(values.reshape(chunk, 4, stored).transpose(1, 0, 2), "row", 0, 0)
            return got.reshape(tokens, stored)

        gathered = lax.all_gather(block_input, "row").transpose(1, 0, 2).reshape(tokens, width)
        gains = lax.all_gather(norm_gains, "row").transpose(1, 0, 2).reshape(4, width)
        tags = lax.ppermute(
            jnp.stack([segment_ids, positions]),
            ("row", "col"),
            [(4 * a + b, 4 * b + a) for a in range(4) for b in range(4)],
        )
        grad_res = wide(to_chunks(cotangent))

        output_t, down_t = output_weight.T, down_weight.T

        def attention_half(j):
            return jnp.concatenate(
                [
                    query_weight[:, j * HEAD_WIDTH : (j + 1) * HEAD_WIDTH],
                    key_matrix,
                    value_matrix,
                    output_t[:, j * HEAD_WIDTH : (j + 1) * HEAD_WIDTH],
                ],
                axis=1,
            )

        def mixed_half(j):
            part = slice(j * half, (j + 1) * half)
            return jnp.concatenate([gate_weight[:, part], up_weight[:, part]], axis=1)

        attention_w = spread(attention_half(0), attention_half(1))
        mixed_w = spread(mixed_half(0), mixed_half(1))
        down_w = spread(down_t[:, :half], down_t[:, half:])

        inverse_one = inverse_rms(wide(gathered))
        normed_one = wide(gathered) * inverse_one
        act_one = low(normed_one * (1.0 + gains[0]))
        cosine, sine = rope_tables(tags[1])
        allowed = visible(tags[0])
        heads = []
        for w in attention_w:
            projected = product(act_one, w[:, : 3 * HEAD_WIDTH])
            query = low(rotate(projected[:, :HEAD_WIDTH], cosine, sine) * scale)
            key = low(rotate(projected[:, HEAD_WIDTH : 2 * HEAD_WIDTH], cosine, sine))
            value = low(projected[:, 2 * HEAD_WIDTH :])
            attended, logsum = attend_forward(query, key, value, allowed)
            heads.append((query, key, value, attended, logsum))
        output_w = jnp.concatenate([w[:, 3 * HEAD_WIDTH :] for w in attention_w], axis=1)
        attended = jnp.concatenate([h[3] for h in heads], axis=1)
        branch_one = scatter_rows(product_nt(attended, output_w))
        residual = wide(lax.dynamic_slice(gathered, (z * chunk, 0), (chunk, width)))
        inverse_b1 = inverse_rms(branch_one)
        hidden_res = residual + branch_one * inverse_b1 * (1.0 + gains[1])
        inverse_two = inverse_rms(hidden_res)
        act_two = gather_rows(hidden_res * inverse_two * (1.0 + gains[2]))

        mixes = []
        for w in mixed_w:
            mixed = product(act_two, w)
            gate, upper = mixed[:, :half], mixed[:, half:]
            activated, gelu_back = jax.vjp(gelu_tanh, gate)
            mixes.append((low(activated * upper), activated, upper, gelu_back))
        branch_two = scatter_rows(sum(product_nt(m[0], w) for m, w in zip(mixes, down_w)))
        inverse_b2 = inverse_rms(branch_two)
        layer_output = from_chunks(low(hidden_res + branch_two * inverse_b2 * (1.0 + gains[3])))

        grad_b2, gain_three = norm_backward(branch_two, inverse_b2, gains[3], grad_res)
        low_two = gather_rows(grad_b2)
        mixed_grads, grad_act_two = [], 0.0
        for m, w, wd in zip(mixes, mixed_w, down_w):
            inner, activated, upper, gelu_back = m
            grad_inner = product(low_two, wd)
            grad_gate = gelu_back(grad_inner * upper)[0]
            grad_mixed = jnp.concatenate([low(grad_gate), low(grad_inner * activated)], axis=1)
            mixed_grads.append(grad_mixed)
            grad_act_two = grad_act_two + product_nt(grad_mixed, w)
        down_grads = collect(*(low(product_tn(low_two, m[0])) for m in mixes))
        grad_act_two = scatter_rows(grad_act_two)
        mixed_w_grads = collect(*(low(product_tn(act_two, g)) for g in mixed_grads))
        grad_hidden, gain_two = norm_backward(hidden_res, inverse_two, gains[2], grad_act_two)
        grad_hidden = grad_hidden + grad_res
        grad_b1, gain_one = norm_backward(branch_one, inverse_b1, gains[1], grad_hidden)

        low_one = gather_rows(grad_b1)
        grad_hidden_local = wide(from_chunks(low(grad_hidden)))
        grad_attended = low(product(low_one, output_w))
        output_grads = low(product_tn(low_one, attended))
        attention_grads, grad_act_one = [], 0.0
        for i, (w, (query, key, value, _, logsum)) in enumerate(zip(attention_w, heads)):
            part = slice(i * HEAD_WIDTH, (i + 1) * HEAD_WIDTH)
            grad_q, grad_k, grad_v = attend_backward(query, key, value, allowed, logsum, grad_attended[:, part])
            grad_qkv = jnp.concatenate(
                [low(rotate(grad_q, cosine, -sine) * scale), low(rotate(grad_k, cosine, -sine)), low(grad_v)], axis=1
            )
            grad_act_one = grad_act_one + product_nt(grad_qkv, w[:, : 3 * HEAD_WIDTH])
            attention_grads.append(jnp.concatenate([low(product_tn(act_one, grad_qkv)), output_grads[:, part]], axis=1))

        normed_grad = grad_act_one * normed_one
        inner_products = lax.psum(jnp.sum(normed_grad * (1.0 + gains[0]), axis=1), "row")
        gain_zero = jnp.sum(normed_grad, axis=0)
        grad_local = wide(
            lax.psum_scatter(
                low(grad_act_one).reshape(tokens, 4, stored).transpose(1, 0, 2), "row", scatter_dimension=0, tiled=False
            )
        )
        attention_w_grads = collect(*attention_grads)
        values = wide(block_input)
        grad_input = grad_hidden_local + inverse_one * (
            grad_local * (1.0 + norm_gains[0]) - values * inverse_one * inner_products[:, None] / width
        )

        gains_total = lax.psum(jnp.stack([gain_zero, gain_one, gain_two, gain_three]), ("dp", "row", "col"))
        gains_total = lax.dynamic_slice(gains_total, (0, z * stored), (4, stored))

        h = HEAD_WIDTH
        a0, a1 = wide(attention_w_grads[0]), wide(attention_w_grads[1])
        m0, m1 = wide(mixed_w_grads[0]), wide(mixed_w_grads[1])
        return (
            layer_output,
            grad_input,
            jnp.concatenate([a0[:, :h], a1[:, :h]], axis=1),
            a0[:, h : 2 * h] + a1[:, h : 2 * h],
            a0[:, 2 * h : 3 * h] + a1[:, 2 * h : 3 * h],
            jnp.concatenate([a0[:, 3 * h :], a1[:, 3 * h :]], axis=1).T,
            jnp.concatenate([m0[:, :half], m1[:, :half]], axis=1),
            jnp.concatenate([m0[:, half:], m1[:, half:]], axis=1),
            jnp.concatenate([wide(down_grads[0]), wide(down_grads[1])], axis=1).T,
            gains_total,
        )

    return body


def solution(mesh):
    return jax.shard_map(
        make_body(mesh.shape["dp"]),
        mesh=mesh,
        in_specs=(
            P(("dp", "col"), "row"),
            P("row", "col"),
            P("row", "col"),
            P("row", "col"),
            P("col", "row"),
            P("row", "col"),
            P("row", "col"),
            P("col", "row"),
            P(None, "row"),
            P(("dp", "row")),
            P(("dp", "row")),
            P(("dp", "col"), "row"),
        ),
        out_specs=(
            P(("dp", "col"), "row"),
            P(("dp", "col"), "row"),
            P("row", "col"),
            P("row", "col"),
            P("row", "col"),
            P("col", "row"),
            P("row", "col"),
            P("row", "col"),
            P("col", "row"),
            P(None, "row"),
        ),
        check_vma=False,
    )
```

```python
import math

import jax
import jax.numpy as jnp
from jax import lax
from jax.sharding import PartitionSpec as P

HEAD_WIDTH = 256
SEQUENCE_LENGTH = 512

EPSILON = 1e-06
SOFT_CAP = 50.0


CORE_SWAP = [(0, 1), (1, 0), (2, 3), (3, 2)]
Y_SWAP = [(0, 2), (2, 0), (1, 3), (3, 1)]
RING = [(0, 1), (1, 2), (2, 3), (3, 0)]


def spread_pairs(phase):
    pairs = []
    for z in range(4):
        for c in range(4):
            y, k = c >> 1, c & 1
            target = 2 * k + (phase ^ (z & 1))
            pairs.append((4 * z + c, 4 * target + 2 * y + (z >> 1)))
    return pairs


SPREAD = [spread_pairs(0), spread_pairs(1)]
COLLECT = [[(b, a) for a, b in pairs] for pairs in SPREAD]


def product(left, right):
    return jnp.dot(left, right, preferred_element_type=jnp.float32)


def product_tn(left, right):
    return lax.dot_general(left, right, (((0,), (0,)), ((), ())), preferred_element_type=jnp.float32)


def product_nt(left, right):
    return lax.dot_general(left, right, (((1,), (1,)), ((), ())), preferred_element_type=jnp.float32)


def low(values):
    return values.astype(jnp.bfloat16)


def wide(values):
    return values.astype(jnp.float32)


def ordered(flag, own, other):
    first = jnp.where(flag == 0, own, other)
    second = jnp.where(flag == 0, other, own)
    return jnp.stack([first, second])


def inverse_rms(values):
    return lax.rsqrt(jnp.mean(values * values, axis=-1, keepdims=True) + EPSILON)


def norm_backward(values, inverse, gain, grad):
    normed = values * inverse
    scaled = grad * (1.0 + gain)
    result = inverse * (scaled - normed * jnp.mean(scaled * normed, axis=-1, keepdims=True))
    return result, jnp.sum(grad * normed, axis=0)


def gelu_tanh(values):
    return jax.nn.gelu(values, approximate=True)


def rope_tables(positions):
    halfway = HEAD_WIDTH // 2
    frequency = jnp.exp(jnp.arange(halfway, dtype=jnp.float32) * (-2.0 * math.log(10000.0) / HEAD_WIDTH))
    angles = positions.astype(jnp.float32)[:, None] * frequency[None, :]
    return jnp.cos(angles), jnp.sin(angles)


def rotate(values, cosine, sine):
    halfway = HEAD_WIDTH // 2
    a, b = values[:, :halfway], values[:, halfway:]
    return jnp.concatenate([a * cosine - b * sine, b * cosine + a * sine], axis=-1)


def visible(segments, ordinal):
    return (ordinal[None, :] <= ordinal[:, None]) & (segments[:, None] == segments[None, :])


def attend_forward(query, key, value, allowed):
    capped = SOFT_CAP * jnp.tanh(product_nt(query, key) / SOFT_CAP)
    totals = jnp.sum(jnp.where(allowed, jnp.exp(capped), 0.0), axis=-1, keepdims=True)
    logsum = jnp.log(totals)
    probs_low = low(jnp.where(allowed, jnp.exp(capped - logsum), 0.0))
    return low(product(probs_low, value)), logsum


def attend_backward(query, key, value, allowed, logsum, grad_out):
    capped = SOFT_CAP * jnp.tanh(product_nt(query, key) / SOFT_CAP)
    probs = jnp.where(allowed, jnp.exp(capped - logsum), 0.0)
    grad_probs = product_nt(grad_out, value)
    centre = jnp.sum(probs * grad_probs, axis=-1, keepdims=True)
    squash = capped / SOFT_CAP
    grad_scores = low(probs * (grad_probs - centre) * (1.0 - squash * squash))
    return product(grad_scores, key), product_tn(grad_scores, query), product_tn(low(probs), grad_out)


def make_body(dp_size):
    def place():
        c = lax.axis_index("col")
        return lax.axis_index("dp"), lax.axis_index("row"), c >> 1, c & 1

    def y_swap(values):
        return lax.ppermute(values, "col", Y_SWAP)

    def core_swap(values):
        return lax.ppermute(values, "col", CORE_SWAP)

    def shift(values):
        return lax.ppermute(values, "row", RING)

    def dp_gather(piece):
        if dp_size == 2:
            other = lax.ppermute(piece, "dp", [(0, 1), (1, 0)])
            return jnp.moveaxis(ordered(lax.axis_index("dp"), piece, other), 0, 1)
        return jnp.moveaxis(lax.all_gather(piece, "dp"), 0, 1)

    def dp_scatter(blocks):
        if dp_size == 2:
            d = lax.axis_index("dp")
            sent = lax.dynamic_index_in_dim(blocks, 1 - d, 1, keepdims=False)
            kept = lax.dynamic_index_in_dim(blocks, d, 1, keepdims=False)
            return low(wide(kept) + wide(lax.ppermute(sent, "dp", [(0, 1), (1, 0)])))
        return lax.psum_scatter(jnp.moveaxis(blocks, 1, 0), "dp", scatter_dimension=0, tiled=False)

    def spread(half_zero, half_one):
        d, z, y, k = place()
        stored, n = half_zero.shape
        rows = stored // dp_size
        halves = jnp.stack([half_zero, half_one])
        parity = z & 1
        got = []
        for phase in range(2):
            piece = lax.dynamic_slice(halves, (phase ^ parity, d * rows, 0), (1, rows, n))[0]
            got.append(lax.ppermute(piece, ("row", "col"), SPREAD[phase]))
        blocks = ordered(parity, got[0], got[1])
        blocks = dp_gather(blocks).reshape(2 * stored, n)
        return ordered(k, blocks, core_swap(blocks)).reshape(4 * stored, n)

    def collect(grads):
        d, z, y, k = place()
        total, n = grads.shape
        stored = total // 4
        rows = stored // dp_size
        both = grads.reshape(2, 2 * stored, n)
        sent = lax.dynamic_index_in_dim(both, 1 - k, 0, keepdims=False)
        kept = lax.dynamic_index_in_dim(both, k, 0, keepdims=False)
        summed = low(wide(kept) + wide(core_swap(sent)))
        pieces = dp_scatter(summed.reshape(2, dp_size, rows, n))
        parity = z & 1
        got = []
        for phase in range(2):
            piece = lax.dynamic_index_in_dim(pieces, phase ^ parity, 0, keepdims=False)
            got.append(lax.ppermute(piece, ("row", "col"), COLLECT[phase]))
        return dp_gather(ordered(parity, got[0], got[1])).reshape(2, stored, n)

    def gather(values):
        own, pairs = low(values), []
        for s in range(4):
            other = y_swap(own)
            pairs.append(jnp.concatenate([own, other], axis=0))
            if s < 3:
                own = shift(own)
        return pairs

    def scatter(parts):
        chunk = parts[0].shape[0] // 2
        summed = {s: parts[s][:chunk] + wide(y_swap(low(parts[s][chunk:]))) for s in (1, 2, 3, 0)}
        total = summed[1]
        for s in (2, 3, 0):
            total = summed[s] + wide(shift(low(total)))
        return total

    def body(
        block_input,
        query_weight,
        key_matrix,
        value_matrix,
        output_weight,
        gate_weight,
        up_weight,
        down_weight,
        norm_gains,
        segment_ids,
        positions,
        cotangent,
    ):
        tokens, stored = block_input.shape
        width = 4 * stored
        chunk = tokens // 4
        scale = HEAD_WIDTH ** (-0.5)
        half = gate_weight.shape[1] // 2
        d, z, y, k = place()

        def to_chunks(values):
            got = lax.all_to_all(values.reshape(4, chunk, stored), "row", 0, 0)
            return got.transpose(1, 0, 2).reshape(chunk, width)

        def from_chunks(values):
            got = lax.all_to_all(values.reshape(chunk, 4, stored).transpose(1, 0, 2), "row", 0, 0)
            return got.reshape(tokens, stored)

        def sequences(pairs):
            return [jnp.concatenate([p[i * chunk : (i + 1) * chunk] for p in pairs], axis=0) for i in range(2)]

        def pairs_of(two):
            return [jnp.concatenate([v[s * chunk : (s + 1) * chunk] for v in two], axis=0) for s in range(4)]

        residual = wide(to_chunks(block_input))
        gains = [norm_gains]
        for _ in range(3):
            gains.append(shift(gains[-1]))
        gains = jnp.stack(gains)
        gains = jnp.concatenate([lax.dynamic_index_in_dim(gains, (z - b) & 3, 0, keepdims=False) for b in range(4)], axis=1)
        tags = lax.ppermute(
            jnp.stack([segment_ids, positions]),
            ("row", "col"),
            [(4 * a + b, 4 * b + a) for a in range(4) for b in range(4)],
        )
        tags = jnp.stack([tags, y_swap(tags)]).reshape(2, 2, 4, chunk)
        order = [(z - s) & 3 for s in range(4)]
        tags = jnp.stack([lax.dynamic_index_in_dim(tags, o, 2, keepdims=False) for o in order], axis=2)
        tags = tags.reshape(2, 2, tokens)
        ordinal = jnp.concatenate([o * chunk + jnp.arange(chunk) for o in order])
        grad_res = wide(to_chunks(cotangent))

        output_t, down_t = output_weight.T, down_weight.T

        def attention_half(j):
            part = slice(j * HEAD_WIDTH, (j + 1) * HEAD_WIDTH)
            return jnp.concatenate([query_weight[:, part], key_matrix, value_matrix, output_t[:, part]], axis=1)

        def mixed_half(j):
            part = slice(j * half, (j + 1) * half)
            return jnp.concatenate([gate_weight[:, part], up_weight[:, part]], axis=1)

        attention_w = spread(attention_half(0), attention_half(1))
        qkv_w, output_w = attention_w[:, : 3 * HEAD_WIDTH], attention_w[:, 3 * HEAD_WIDTH :]
        mixed_w = spread(mixed_half(0), mixed_half(1))
        down_w = spread(down_t[:, :half], down_t[:, half:])

        inverse_one = inverse_rms(residual)
        act_one = gather(residual * inverse_one * (1.0 + gains[0]))
        heads = []
        for i, projected in enumerate(sequences([product(a, qkv_w) for a in act_one])):
            cosine, sine = rope_tables(tags[i, 1])
            allowed = visible(tags[i, 0], ordinal)
            query = low(rotate(projected[:, :HEAD_WIDTH], cosine, sine) * scale)
            key = low(rotate(projected[:, HEAD_WIDTH : 2 * HEAD_WIDTH], cosine, sine))
            value = low(projected[:, 2 * HEAD_WIDTH :])
            attended, logsum = attend_forward(query, key, value, allowed)
            heads.append((query, key, value, allowed, attended, logsum, cosine, sine))
        attended = pairs_of([h[4] for h in heads])
        branch_one = scatter([product_nt(a, output_w) for a in attended])
        inverse_b1 = inverse_rms(branch_one)
        hidden_res = residual + branch_one * inverse_b1 * (1.0 + gains[1])
        inverse_two = inverse_rms(hidden_res)

        act_two = gather(hidden_res * inverse_two * (1.0 + gains[2]))
        mixes = []
        for a in act_two:
            mixed = product(a, mixed_w)
            gate, upper = mixed[:, :half], mixed[:, half:]
            activated, gelu_back = jax.vjp(gelu_tanh, gate)
            mixes.append((low(activated * upper), activated, upper, gelu_back))
        branch_two = scatter([product_nt(m[0], down_w) for m in mixes])
        inverse_b2 = inverse_rms(branch_two)
        layer_output = from_chunks(low(hidden_res + branch_two * inverse_b2 * (1.0 + gains[3])))

        grad_b2, gain_three = norm_backward(branch_two, inverse_b2, gains[3], grad_res)
        low_two = gather(grad_b2)
        mixed_grads = []
        for g, (_, activated, upper, gelu_back) in zip(low_two, mixes):
            grad_inner = product(g, down_w)
            grad_gate = gelu_back(grad_inner * upper)[0]
            mixed_grads.append(jnp.concatenate([low(grad_gate), low(grad_inner * activated)], axis=1))
        grad_act_two = scatter([product_nt(g, mixed_w) for g in mixed_grads])
        down_grads = collect(low(product_tn(jnp.concatenate(low_two), jnp.concatenate([m[0] for m in mixes]))))
        mixed_w_grads = collect(low(product_tn(jnp.concatenate(act_two), jnp.concatenate(mixed_grads))))
        grad_hidden, gain_two = norm_backward(hidden_res, inverse_two, gains[2], grad_act_two)
        grad_hidden = grad_hidden + grad_res
        grad_b1, gain_one = norm_backward(branch_one, inverse_b1, gains[1], grad_hidden)

        low_one = gather(grad_b1)
        grad_attended = sequences([low(product(g, output_w)) for g in low_one])
        grad_qkv = []
        for (query, key, value, allowed, _, logsum, cosine, sine), grad_out in zip(heads, grad_attended):
            grad_q, grad_k, grad_v = attend_backward(query, key, value, allowed, logsum, grad_out)
            grad_q, grad_k = rotate(grad_q, cosine, -sine) * scale, rotate(grad_k, cosine, -sine)
            grad_qkv.append(jnp.concatenate([low(grad_q), low(grad_k), low(grad_v)], axis=1))
        grad_qkv = pairs_of(grad_qkv)
        grad_act_one = scatter([product_nt(g, qkv_w) for g in grad_qkv])
        qkv_grads = low(product_tn(jnp.concatenate(act_one), jnp.concatenate(grad_qkv)))
        output_grads = low(product_tn(jnp.concatenate(low_one), jnp.concatenate(attended)))
        attention_w_grads = collect(jnp.concatenate([qkv_grads, output_grads], axis=1))
        grad_input, gain_zero = norm_backward(residual, inverse_one, gains[0], grad_act_one)
        grad_input = wide(from_chunks(low(grad_input + grad_hidden)))

        gains_total = jnp.stack([gain_zero, gain_one, gain_two, gain_three])
        gains_total = gains_total + core_swap(gains_total)
        gains_total = gains_total + y_swap(gains_total)
        if dp_size == 2:
            gains_total = gains_total + lax.ppermute(gains_total, "dp", [(0, 1), (1, 0)])
        else:
            gains_total = lax.psum(gains_total, "dp")
        blocks = gains_total.reshape(4, 4, stored).transpose(1, 0, 2)
        gains_total = lax.dynamic_index_in_dim(blocks, z, 0, keepdims=False)
        for step in range(1, 4):
            sent = lax.dynamic_index_in_dim(blocks, (z + step) & 3, 0, keepdims=False)
            gains_total = gains_total + lax.ppermute(sent, "row", [(a, (a + step) & 3) for a in range(4)])

        h = HEAD_WIDTH
        a0, a1 = wide(attention_w_grads[0]), wide(attention_w_grads[1])
        m0, m1 = wide(mixed_w_grads[0]), wide(mixed_w_grads[1])
        return (
            layer_output,
            grad_input,
            jnp.concatenate([a0[:, :h], a1[:, :h]], axis=1),
            a0[:, h : 2 * h] + a1[:, h : 2 * h],
            a0[:, 2 * h : 3 * h] + a1[:, 2 * h : 3 * h],
            jnp.concatenate([a0[:, 3 * h :], a1[:, 3 * h :]], axis=1).T,
            jnp.concatenate([m0[:, :half], m1[:, :half]], axis=1),
            jnp.concatenate([m0[:, half:], m1[:, half:]], axis=1),
            jnp.concatenate([wide(down_grads[0]), wide(down_grads[1])], axis=1).T,
            gains_total,
        )

    return body


def solution(mesh):
    return jax.shard_map(
        make_body(mesh.shape["dp"]),
        mesh=mesh,
        in_specs=(
            P(("dp", "col"), "row"),
            P("row", "col"),
            P("row", "col"),
            P("row", "col"),
            P("col", "row"),
            P("row", "col"),
            P("row", "col"),
            P("col", "row"),
            P(None, "row"),
            P(("dp", "row")),
            P(("dp", "row")),
            P(("dp", "col"), "row"),
        ),
        out_specs=(
            P(("dp", "col"), "row"),
            P(("dp", "col"), "row"),
            P("row", "col"),
            P("row", "col"),
            P("row", "col"),
            P("col", "row"),
            P("row", "col"),
            P("row", "col"),
            P("col", "row"),
            P(None, "row"),
        ),
        check_vma=False,
    )
```

```python
import math

import jax
import jax.numpy as jnp
from jax import lax
from jax.sharding import PartitionSpec as P


HEAD_WIDTH = 256

EPSILON = 1e-06
SOFT_CAP = 50.0


CORE_SWAP = [(0, 1), (1, 0), (2, 3), (3, 2)]
Y_SWAP = [(0, 2), (2, 0), (1, 3), (3, 1)]
RING = [(0, 1), (1, 2), (2, 3), (3, 0)]


def spread_pairs(phase):
    pairs = []
    for z in range(4):
        for c in range(4):
            y, k = c >> 1, c & 1
            target = 2 * k + (phase ^ (z & 1))
            pairs.append((4 * z + c, 4 * target + 2 * y + (z >> 1)))
    return pairs


SPREAD = [spread_pairs(0), spread_pairs(1)]
COLLECT = [[(b, a) for a, b in pairs] for pairs in SPREAD]


def product(left, right):
    return jnp.dot(left, right, preferred_element_type=jnp.float32)


def product_tn(left, right):
    return lax.dot_general(left, right, (((0,), (0,)), ((), ())), preferred_element_type=jnp.float32)


def product_nt(left, right):
    return lax.dot_general(left, right, (((1,), (1,)), ((), ())), preferred_element_type=jnp.float32)


def low(values):
    return values.astype(jnp.bfloat16)


def wide(values):
    return values.astype(jnp.float32)


def ordered(flag, own, other):
    first = jnp.where(flag == 0, own, other)
    second = jnp.where(flag == 0, other, own)
    return jnp.stack([first, second])


def inverse_rms(values):
    return lax.rsqrt(jnp.mean(values * values, axis=-1, keepdims=True) + EPSILON)


def norm_backward(values, inverse, gain, grad):
    normed = values * inverse
    scaled = grad * (1.0 + gain)
    result = inverse * (scaled - normed * jnp.mean(scaled * normed, axis=-1, keepdims=True))
    return result, jnp.sum(grad * normed, axis=0)


def gelu_tanh(values):
    return jax.nn.gelu(values, approximate=True)


def rope_tables(positions):
    halfway = HEAD_WIDTH // 2
    frequency = jnp.exp(jnp.arange(halfway, dtype=jnp.float32) * (-2.0 * math.log(10000.0) / HEAD_WIDTH))
    angles = positions.astype(jnp.float32)[:, None] * frequency[None, :]
    return jnp.cos(angles), jnp.sin(angles)


def rotate(values, cosine, sine):
    halfway = HEAD_WIDTH // 2
    a, b = values[:, :halfway], values[:, halfway:]
    return jnp.concatenate([a * cosine - b * sine, b * cosine + a * sine], axis=-1)


def visible(segments, ordinal):
    return (ordinal[None, :] <= ordinal[:, None]) & (segments[:, None] == segments[None, :])


def attend_forward(query, key, value, allowed):
    capped = SOFT_CAP * jnp.tanh(product_nt(query, key) / SOFT_CAP)
    totals = jnp.sum(jnp.where(allowed, jnp.exp(capped), 0.0), axis=-1, keepdims=True)
    logsum = jnp.log(totals)
    probs_low = low(jnp.where(allowed, jnp.exp(capped - logsum), 0.0))
    return low(product(probs_low, value)), logsum


def attend_backward(query, key, value, allowed, logsum, grad_out):
    capped = SOFT_CAP * jnp.tanh(product_nt(query, key) / SOFT_CAP)
    probs = jnp.where(allowed, jnp.exp(capped - logsum), 0.0)
    grad_probs = product_nt(grad_out, value)
    centre = jnp.sum(probs * grad_probs, axis=-1, keepdims=True)
    squash = capped / SOFT_CAP
    grad_scores = low(probs * (grad_probs - centre) * (1.0 - squash * squash))
    return product(grad_scores, key), product_tn(grad_scores, query), product_tn(low(probs), grad_out)


def make_body(dp_size):
    def place():
        c = lax.axis_index("col")
        return lax.axis_index("dp"), lax.axis_index("row"), c >> 1, c & 1

    def y_swap(values):
        return lax.ppermute(values, "col", Y_SWAP)

    def core_swap(values):
        return lax.ppermute(values, "col", CORE_SWAP)

    def shift(values):
        return lax.ppermute(values, "row", RING)

    def dp_gather(piece):
        if dp_size == 2:
            other = lax.ppermute(piece, "dp", [(0, 1), (1, 0)])
            return ordered(lax.axis_index("dp"), piece, other)
        return lax.all_gather(piece, "dp")

    def dp_scatter(blocks):
        if dp_size == 2:
            d = lax.axis_index("dp")
            sent = lax.dynamic_index_in_dim(blocks, 1 - d, 0, keepdims=False)
            kept = lax.dynamic_index_in_dim(blocks, d, 0, keepdims=False)
            other = lax.ppermute(sent, "dp", [(0, 1), (1, 0)])
            return low(wide(kept) + wide(other))
        return lax.psum_scatter(blocks, "dp", scatter_dimension=0, tiled=False)

    def spread(half_zero, half_one):
        d, z, _, k = place()
        stored, n = half_zero.shape
        rows = stored // dp_size
        halves = jnp.stack([half_zero, half_one])
        parity = z & 1
        got = []
        for phase in range(2):
            piece = lax.dynamic_slice(halves, (phase ^ parity, d * rows, 0), (1, rows, n))[0]
            piece = lax.ppermute(piece, ("row", "col"), SPREAD[phase])
            got.append(dp_gather(piece).reshape(stored, n))
        blocks = ordered(parity, got[0], got[1]).reshape(2 * stored, n)
        other = core_swap(blocks)
        return ordered(k, blocks, other).reshape(4 * stored, n)

    def collect(grads):
        _, z, _, k = place()
        total, n = grads.shape
        stored = total // 4
        rows = stored // dp_size
        both = grads.reshape(2, 2 * stored, n)
        sent = lax.dynamic_index_in_dim(both, 1 - k, 0, keepdims=False)
        kept = lax.dynamic_index_in_dim(both, k, 0, keepdims=False)
        other = core_swap(sent)
        summed = low(wide(kept) + wide(other)).reshape(2, dp_size, rows, n)
        parity = z & 1
        got = []
        for phase in range(2):
            piece = lax.dynamic_index_in_dim(summed, phase ^ parity, 0, keepdims=False)
            piece = dp_scatter(piece)
            piece = lax.ppermute(piece, ("row", "col"), COLLECT[phase])
            got.append(dp_gather(piece).reshape(stored, n))
        return ordered(parity, got[0], got[1])

    def gather(values):
        own, pairs = low(values), []
        for s in range(4):
            other = y_swap(own)
            pairs.append(jnp.concatenate([own, other], axis=0))
            if s < 3:
                own = shift(own)
        return pairs

    def scatter(parts):
        chunk = parts[0].shape[0] // 2
        summed = {s: parts[s][:chunk] + wide(y_swap(low(parts[s][chunk:]))) for s in (1, 2, 3, 0)}
        total = summed[1]
        for s in (2, 3, 0):
            total = summed[s] + wide(shift(low(total)))
        return total

    def products(operation, pairs, weight):
        out = []
        for values in pairs:
            out.append(operation(values, weight))
        return out

    def layer(
        block_input,
        query_weight,
        key_matrix,
        value_matrix,
        output_weight,
        gate_weight,
        up_weight,
        down_weight,
        norm_gains,
        segment_ids,
        positions,
        cotangent,
    ):
        tokens, stored = block_input.shape
        chunk = tokens // 4
        scale = HEAD_WIDTH ** (-0.5)
        half = gate_weight.shape[1] // 2
        _, z, _, _ = place()

        def exchange(blocks):
            got = [lax.dynamic_index_in_dim(blocks, z, 0, keepdims=False)]
            for step in range(1, 4):
                sent = lax.dynamic_index_in_dim(blocks, (z + step) & 3, 0, keepdims=False)
                got.append(lax.ppermute(sent, "row", [(a, (a + step) & 3) for a in range(4)]))
            got = jnp.stack(got)
            return [lax.dynamic_index_in_dim(got, (z - b) & 3, 0, keepdims=False) for b in range(4)]

        def to_chunks(values):
            return jnp.concatenate(exchange(values.reshape(4, chunk, stored)), axis=1)

        def from_chunks(values):
            blocks = values.reshape(chunk, 4, stored).transpose(1, 0, 2)
            return jnp.concatenate(exchange(blocks), axis=0)

        def sequences(pairs):
            return [jnp.concatenate([p[i * chunk : (i + 1) * chunk] for p in pairs], axis=0) for i in range(2)]

        def pairs_of(two):
            return [jnp.concatenate([v[s * chunk : (s + 1) * chunk] for v in two], axis=0) for s in range(4)]

        residual = wide(to_chunks(block_input))
        gains = jnp.concatenate(exchange(jnp.broadcast_to(norm_gains, (4, 4, stored))), axis=1)
        tags = lax.ppermute(
            jnp.stack([segment_ids, positions]),
            ("row", "col"),
            [(4 * a + b, 4 * b + a) for a in range(4) for b in range(4)],
        )
        tags = jnp.stack([tags, y_swap(tags)]).reshape(2, 2, 4, chunk)
        order = [(z - s) & 3 for s in range(4)]
        tags = jnp.stack([lax.dynamic_index_in_dim(tags, o, 2, keepdims=False) for o in order], axis=2)
        tags = tags.reshape(2, 2, tokens)
        ordinal = jnp.concatenate([o * chunk + jnp.arange(chunk) for o in order])
        grad_res = wide(to_chunks(cotangent))

        output_t, down_t = output_weight.T, down_weight.T

        def attention_half(j):
            part = slice(j * HEAD_WIDTH, (j + 1) * HEAD_WIDTH)
            return jnp.concatenate([query_weight[:, part], key_matrix, value_matrix, output_t[:, part]], axis=1)

        def mixed_half(j):
            part = slice(j * half, (j + 1) * half)
            return jnp.concatenate([gate_weight[:, part], up_weight[:, part]], axis=1)

        attention_w = spread(attention_half(0), attention_half(1))
        qkv_w, output_w = attention_w[:, : 3 * HEAD_WIDTH], attention_w[:, 3 * HEAD_WIDTH :]
        mixed_w = spread(mixed_half(0), mixed_half(1))
        down_w = spread(down_t[:, :half], down_t[:, half:])

        inverse_one = inverse_rms(residual)
        act_one = gather(residual * inverse_one * (1.0 + gains[0]))
        heads = []
        for i, projected in enumerate(sequences(products(product, act_one, qkv_w))):
            cosine, sine = rope_tables(tags[i, 1])
            allowed = visible(tags[i, 0], ordinal)
            query = low(rotate(projected[:, :HEAD_WIDTH], cosine, sine) * scale)
            key = low(rotate(projected[:, HEAD_WIDTH : 2 * HEAD_WIDTH], cosine, sine))
            value = low(projected[:, 2 * HEAD_WIDTH :])
            attended, logsum = attend_forward(query, key, value, allowed)
            heads.append((query, key, value, allowed, attended, logsum, cosine, sine))
        attended = pairs_of([h[4] for h in heads])
        branch_one = scatter(products(product_nt, attended, output_w))
        inverse_b1 = inverse_rms(branch_one)
        hidden_res = residual + branch_one * inverse_b1 * (1.0 + gains[1])
        inverse_two = inverse_rms(hidden_res)

        act_two = gather(hidden_res * inverse_two * (1.0 + gains[2]))
        mixes = []
        for mixed in products(product, act_two, mixed_w):
            gate, upper = mixed[:, :half], mixed[:, half:]
            activated, gelu_back = jax.vjp(gelu_tanh, gate)
            mixes.append((low(activated * upper), activated, upper, gelu_back))
        branch_two = scatter(products(product_nt, [m[0] for m in mixes], down_w))
        inverse_b2 = inverse_rms(branch_two)
        layer_output = from_chunks(low(hidden_res + branch_two * inverse_b2 * (1.0 + gains[3])))

        grad_b2, gain_three = norm_backward(branch_two, inverse_b2, gains[3], grad_res)
        low_two = gather(grad_b2)
        mixed_grads = []
        for g, (_, activated, upper, gelu_back) in zip(low_two, mixes):
            grad_inner = product(g, down_w)
            grad_gate = gelu_back(grad_inner * upper)[0]
            mixed_grads.append(jnp.concatenate([low(grad_gate), low(grad_inner * activated)], axis=1))
        grad_act_two = scatter(products(product_nt, mixed_grads, mixed_w))
        down_grads = low(product_tn(jnp.concatenate(low_two), jnp.concatenate([m[0] for m in mixes])))
        down_grads = collect(down_grads)
        mixed_w_grads = low(product_tn(jnp.concatenate(act_two), jnp.concatenate(mixed_grads)))
        mixed_w_grads = collect(mixed_w_grads)
        grad_hidden, gain_two = norm_backward(hidden_res, inverse_two, gains[2], grad_act_two)
        grad_hidden = grad_hidden + grad_res
        grad_b1, gain_one = norm_backward(branch_one, inverse_b1, gains[1], grad_hidden)

        low_one = gather(grad_b1)
        grad_attended = sequences([low(g) for g in products(product, low_one, output_w)])
        grad_qkv = []
        for (query, key, value, allowed, _, logsum, cosine, sine), grad_out in zip(heads, grad_attended):
            grad_q, grad_k, grad_v = attend_backward(query, key, value, allowed, logsum, grad_out)
            grad_q, grad_k = rotate(grad_q, cosine, -sine) * scale, rotate(grad_k, cosine, -sine)
            grad_qkv.append(jnp.concatenate([low(grad_q), low(grad_k), low(grad_v)], axis=1))
        grad_qkv = pairs_of(grad_qkv)
        grad_act_one = scatter(products(product_nt, grad_qkv, qkv_w))
        qkv_grads = low(product_tn(jnp.concatenate(act_one), jnp.concatenate(grad_qkv)))
        output_grads = low(product_tn(jnp.concatenate(low_one), jnp.concatenate(attended)))
        attention_w_grads = collect(jnp.concatenate([qkv_grads, output_grads], axis=1))
        grad_input, gain_zero = norm_backward(residual, inverse_one, gains[0], grad_act_one)
        grad_input = wide(from_chunks(low(grad_input + grad_hidden)))

        gains_total = jnp.stack([gain_zero, gain_one, gain_two, gain_three])
        gains_total = gains_total + core_swap(gains_total)
        gains_total = gains_total + y_swap(gains_total)
        if dp_size == 2:
            gains_total = gains_total + lax.ppermute(gains_total, "dp", [(0, 1), (1, 0)])
        else:
            gains_total = lax.psum(gains_total, "dp")
        gains_total = sum(exchange(gains_total.reshape(4, 4, stored).transpose(1, 0, 2)))

        h = HEAD_WIDTH
        a0, a1 = wide(attention_w_grads[0]), wide(attention_w_grads[1])
        m0, m1 = wide(mixed_w_grads[0]), wide(mixed_w_grads[1])
        return (
            layer_output,
            grad_input,
            jnp.concatenate([a0[:, :h], a1[:, :h]], axis=1),
            a0[:, h : 2 * h] + a1[:, h : 2 * h],
            a0[:, 2 * h : 3 * h] + a1[:, 2 * h : 3 * h],
            jnp.concatenate([a0[:, 3 * h :], a1[:, 3 * h :]], axis=1).T,
            jnp.concatenate([m0[:, :half], m1[:, :half]], axis=1),
            jnp.concatenate([m0[:, half:], m1[:, half:]], axis=1),
            jnp.concatenate([wide(down_grads[0]), wide(down_grads[1])], axis=1).T,
            gains_total,
        )

    return layer


def solution(mesh):
    return jax.shard_map(
        make_body(mesh.shape["dp"]),
        mesh=mesh,
        in_specs=(
            P(("dp", "col"), "row"),
            P("row", "col"),
            P("row", "col"),
            P("row", "col"),
            P("col", "row"),
            P("row", "col"),
            P("row", "col"),
            P("col", "row"),
            P(None, "row"),
            P(("dp", "row")),
            P(("dp", "row")),
            P(("dp", "col"), "row"),
        ),
        out_specs=(
            P(("dp", "col"), "row"),
            P(("dp", "col"), "row"),
            P("row", "col"),
            P("row", "col"),
            P("row", "col"),
            P("col", "row"),
            P("row", "col"),
            P("row", "col"),
            P("col", "row"),
            P(None, "row"),
        ),
        check_vma=False,
    )
```
